32 devices in a mesh: tm: 8 (over y, x, core), sector: 4 (over z).
Axes of the slice: x: 2, y: 2, z: 4, core: 2. Of those that a mesh axis runs over, the one named last changes fastest.
Arguments:
- propagator: bfloat16 [4, 8, 640, 640], P('sector', 'tm'), may hold values from -6 to 6
- rising_op: bfloat16 [4, 640, 640], P('sector'), may hold values from -0.25 to 0.25
- energies: float32 [4, 640], P('sector'), may hold values from 0.5 to 40
- hyb_particle: float32 [8], P('tm'), may hold values from 0.2 to 1
- hyb_hole: float32 [8], P('tm'), may hold values from 0.2 to 1
- sector_sizes: int32 [4], P('sector'), may hold values from 160 to 640, as said below
Outputs:
- new_prop: bfloat16 [4, 8, 640, 640], P('sector', 'tm')
The draws below stay inside these ranges and needn't reach their ends.
Inputs may be any that keep to these rules, and one draw needn't show every extreme that they name: `sector_sizes`: one sector holds exactly 640 states.
All inputs are finite; a program needn't handle non-finite values.
Results may differ from the reference program's by a relative error of at most 0.0061.
Values may be sent and summed in bfloat16 or wider, within the bound.
A program may use at most 128 MiB of HBM per device.

```python
import math
import jax
import jax.numpy as jnp
from jax import lax

B = 640
SECT = 4
TIMES = 8


def draw_sector_sizes(key, part):
    first_key = jax.random.fold_in(key, 11)
    second_key = jax.random.fold_in(key, 12)
    counts_drawn = jax.random.randint(first_key, (SECT,), B // 4, B + 1)
    chosen = jax.random.randint(second_key, (), 0, SECT)
    return jnp.where(jnp.arange(SECT) == chosen, B, counts_drawn).astype(jnp.int32)


def levels(key, shape, split, low, high):
    def one(position, parts):
        draws = jax.random.uniform(jax.random.fold_in(jax.random.fold_in(key, 6), position), (parts,), jnp.float32, low / len(split), high / len(split))
        return jnp.repeat(jnp.exp(draws), shape[position] // parts).reshape((-1,) + (1,) * (len(shape) - position - 1))

    level = one(*split[0])
    for cut in split[1:]:
        level = level * one(*cut)
    return level


def centred(stream_key, shape, deviation, reach, shards=(), kind=jnp.bfloat16):
    result = jax.random.normal(stream_key, shape, jnp.float32) * deviation
    if len(shards) > 0:
        result = levels(stream_key, shape, shards, -0.22, 0.18) * result
    return jnp.clip(result, min=-reach, max=reach).astype(kind)


def setup_inputs(seed: int = 0) -> dict:
    splits = jax.random.split(jax.random.key(seed), 7)
    return {
        "propagator": centred(splits[0], (SECT, TIMES, B, B), 1.0, 6.0, ((0, 4), (1, 8))),
        "rising_op": centred(splits[1], (SECT, B, B), B ** -0.5, 0.25, ((0, 4),)),
        "energies": jnp.clip(jnp.exp(math.log(40.0) - 4.3820266 * jax.random.uniform(splits[2], (SECT, B), jnp.float32) ** levels(splits[2], (SECT, B), ((0, 4),), -0.2, 0.2)), 0.5, 40.0),
        "hyb_particle": jnp.clip(jnp.exp(math.log(1.0) - 1.609438 * jax.random.uniform(splits[3], (TIMES,), jnp.float32) ** levels(splits[3], (TIMES,), ((0, 8),), -0.2, 0.2)), 0.2, 1.0),
        "hyb_hole": jnp.clip(jnp.exp(math.log(1.0) - 1.609438 * jax.random.uniform(splits[4], (TIMES,), jnp.float32) ** levels(splits[4], (TIMES,), ((0, 8),), -0.2, 0.2)), 0.2, 1.0),
        "sector_sizes": draw_sector_sizes(jax.random.fold_in(splits[6], 71), 0),
    }


def reference(propagator, rising_op, energies, hyb_particle, hyb_hole, sector_sizes):
    highest = lax.Precision.HIGHEST
    step_size = 1.0 / TIMES
    positions = jnp.arange(B, dtype=jnp.int32)
    live_mask = positions[None, :] < sector_sizes[:, None]
    square = live_mask[:, :, None] & live_mask[:, None, :]
    masked_prop = jnp.where(square[:, None], propagator, jnp.zeros((), propagator.dtype))
    operator_wide = rising_op.astype(jnp.float32)
    raised = jnp.einsum('sik,stkl->stil', operator_wide, masked_prop.astype(jnp.float32), precision=highest).astype(jnp.bfloat16)
    upward = jnp.einsum('stik,sjk->stij', raised.astype(jnp.float32), operator_wide, precision=highest).astype(jnp.bfloat16)
    from_below = jnp.concatenate([jnp.zeros_like(upward[:1]), upward[:-1]], 0)
    from_above = jnp.concatenate([masked_prop[1:], jnp.zeros_like(masked_prop[:1])], 0)
    lowered = jnp.einsum('ski,stkl->stil', operator_wide, from_above.astype(jnp.float32), precision=highest).astype(jnp.bfloat16)
    downward = jnp.einsum('stik,skl->stil', lowered.astype(jnp.float32), operator_wide, precision=highest)
    combined = hyb_particle[None, :, None, None] * from_below.astype(jnp.float32) + hyb_hole[None, :, None, None] * downward
    self_energy = jnp.where(square[:, None], combined, jnp.zeros((), jnp.float32)).astype(jnp.bfloat16)
    identity = positions[:, None] == positions[None, :]

    def one_sector(operands):
        lag_table, history, level_rates, live_row = operands
        lag_wide = lag_table.astype(jnp.float32)
        history_wide = history.astype(jnp.float32)
        running_sum = jnp.zeros((TIMES, B, B), jnp.float32)
        for lag in range(TIMES):
            running_sum = running_sum.at[lag:].add(jnp.einsum('ik,tkl->til', lag_wide[lag], history_wide[:TIMES - lag], precision=highest))
        convolved = step_size * running_sum
        decay = jnp.exp(-step_size * level_rates)

        def advance(running, term):
            running = decay[:, None] * running + term
            return running, running

        _, summed = lax.scan(advance, jnp.zeros((B, B), jnp.float32), convolved)
        moments = jnp.arange(TIMES).astype(jnp.float32)
        free_part = jnp.where(live_row[None, :], jnp.exp(-level_rates[None, :] * (moments[:, None] * step_size)), jnp.zeros((), jnp.float32))
        diagonal = jnp.where(identity[None], free_part[:, :, None], jnp.zeros((), jnp.float32))
        return (diagonal - step_size * summed).astype(jnp.bfloat16)

    return lax.map(one_sector, (self_energy, masked_prop, energies, live_mask))
```

```python
import functools
import jax
import jax.numpy as jnp
from jax import lax
from jax.experimental import pallas as pl
from jax.experimental.pallas import tpu as pltpu
from jax.sharding import PartitionSpec as P


def shifted(block, axis, distance):
    devices = range(lax.axis_size(axis))
    route = [(i - distance, i) for i in devices if i - distance in devices]
    return lax.ppermute(block, axis, route)


def general_device(propagator, rising_op, energies, hyb_particle, hyb_hole, sector_sizes):
    t_dev = propagator.shape[1]
    states = propagator.shape[2]
    time_count = t_dev * lax.axis_size("tm")
    step_size = 1.0 / time_count
    positions = jnp.arange(states, dtype=jnp.int32)
    live_mask = positions < sector_sizes[0]
    square = live_mask[:, None] & live_mask[None, :]
    masked_prop = jnp.where(square[None], propagator[0], jnp.zeros((), jnp.bfloat16))
    operator = rising_op[0]
    raised = jnp.einsum(
        "ik,tkl->til", operator, masked_prop, preferred_element_type=jnp.float32
    ).astype(jnp.bfloat16)
    upward = jnp.einsum("tik,jk->tij", raised, operator, preferred_element_type=jnp.float32).astype(
        jnp.bfloat16
    )
    from_below = shifted(upward, "sector", 1)
    from_above = shifted(masked_prop, "sector", -1)
    lowered = jnp.einsum(
        "ki,tkl->til", operator, from_above, preferred_element_type=jnp.float32
    ).astype(jnp.bfloat16)
    downward = jnp.einsum("tik,kl->til", lowered, operator, preferred_element_type=jnp.float32)
    combined = (
        hyb_particle[:, None, None] * from_below.astype(jnp.float32)
        + hyb_hole[:, None, None] * downward
    )
    self_energy = jnp.where(square[None], combined, jnp.zeros((), jnp.float32)).astype(jnp.bfloat16)
    rows_each = states // lax.axis_size("tm")
    first_row = lax.axis_index("tm") * rows_each
    lag_rows = lax.all_to_all(self_energy, "tm", split_axis=1, concat_axis=0, tiled=True)
    history = lax.all_gather(masked_prop, "tm", axis=0, tiled=True)
    mirrored = jnp.concatenate([history[::-1], history], 0)
    slots = jnp.arange(time_count, dtype=jnp.int32)
    wide_slots = jnp.arange(time_count + 1, dtype=jnp.int32)

    def pair_step(lag, sums):
        forward, backward = sums
        other = time_count - 1 - lag
        window = lax.dynamic_slice_in_dim(mirrored, lag, time_count + 1, 0)
        near = lax.dynamic_index_in_dim(lag_rows, lag, 0, keepdims=False)
        far = lax.dynamic_index_in_dim(lag_rows, other, 0, keepdims=False)
        left = jnp.where((wide_slots < time_count - lag)[:, None, None], near[None], far[None])
        product = jnp.einsum("uik,ukl->uil", left, window, preferred_element_type=jnp.float32)
        backward = backward + jnp.where(
            (slots < time_count - lag)[:, None, None],
            product[:time_count],
            jnp.zeros((), jnp.float32),
        )
        forward = forward + jnp.where(
            (slots >= time_count - lag - 1)[:, None, None], product[1:], jnp.zeros((), jnp.float32)
        )
        return (forward, backward)

    empty_rows = jnp.zeros((time_count, rows_each, states), jnp.float32)
    forward, backward = lax.fori_loop(0, time_count // 2, pair_step, (empty_rows, empty_rows))
    convolved = step_size * (forward + backward[::-1])
    row_ids = first_row + jnp.arange(rows_each, dtype=jnp.int32)
    row_rates = lax.dynamic_slice_in_dim(energies[0], first_row, rows_each, 0)
    decay_rows = jnp.exp(-step_size * row_rates)

    def advance(running, term):
        running = decay_rows[:, None] * running + term
        return (running, running)

    _, summed = lax.scan(advance, jnp.zeros((rows_each, states), jnp.float32), convolved)
    moments = jnp.arange(time_count).astype(jnp.float32) * step_size
    live_rows = row_ids < sector_sizes[0]
    free_part = jnp.where(
        live_rows[None, :],
        jnp.exp(-row_rates[None, :] * moments[:, None]),
        jnp.zeros((), jnp.float32),
    )
    diagonal = jnp.where(
        (row_ids[:, None] == positions[None, :])[None],
        free_part[:, :, None],
        jnp.zeros((), jnp.float32),
    )
    new_rows = (diagonal - step_size * summed).astype(jnp.bfloat16)
    return lax.all_to_all(new_rows, "tm", split_axis=0, concat_axis=1, tiled=True)[None]


MESH = pl.DeviceIdType.MESH
ROW_TILE = 16
LANES = 128


def flipped(index, mask):
    bit = 1
    while bit <= mask:
        if mask & bit:
            index = index + bit - 2 * bit * lax.rem(lax.div(index, bit), 2)
        bit *= 2
    return index


def last_hops(mask):
    bits = [1 << i for i in range(mask.bit_length()) if mask >> i & 1]
    if bits[0] == 1:
        return (1, 1)
    return (bits[0], bits[-1])


def fused_kernel(
    times,
    sectors,
    size_ref,
    particle_ref,
    hole_ref,
    prop_ref,
    operator_ref,
    energy_ref,
    out_ref,
    history,
    turned,
    upward,
    below,
    above,
    energy_out,
    energy_in,
    sums,
    fresh,
    z_send,
    z_recv,
    gather_send,
    gather_recv,
    rows_send,
    rows_recv,
    out_send,
    out_recv,
):
    states = prop_ref.shape[-1]
    rows = states // times
    half = states // 2
    step_size = 1.0 / times
    me = lax.axis_index("tm")
    sector = lax.axis_index("sector")
    has_below = sector > 0
    has_above = sector < sectors - 1

    barrier = pltpu.get_barrier_semaphore()
    for mask in range(1, times):
        pl.semaphore_signal(
            barrier, inc=1, device_id={"tm": flipped(me, mask)}, device_id_type=MESH
        )

    @pl.when(has_below)
    def _():
        pl.semaphore_signal(barrier, inc=1, device_id={"sector": sector - 1}, device_id_type=MESH)

    @pl.when(has_above)
    def _():
        pl.semaphore_signal(barrier, inc=1, device_id={"sector": sector + 1}, device_id_type=MESH)

    size = size_ref[0]
    live = (lax.broadcasted_iota(jnp.int32, (states, states), 0) < size) & (
        lax.broadcasted_iota(jnp.int32, (states, states), 1) < size
    )
    history[me] = jnp.where(
        live, prop_ref[0, 0].astype(jnp.float32), jnp.zeros((), jnp.float32)
    ).astype(jnp.bfloat16)

    neighbours = jnp.where(has_below, 1, 0) + jnp.where(has_above, 1, 0)
    pl.semaphore_wait(barrier, times - 1 + neighbours)

    def down_copy():
        return pltpu.make_async_remote_copy(
            src_ref=history.at[me],
            dst_ref=above,
            send_sem=z_send.at[0],
            recv_sem=z_recv.at[0],
            device_id={"sector": sector - 1},
            device_id_type=MESH,
        )

    def up_copy():
        return pltpu.make_async_remote_copy(
            src_ref=upward,
            dst_ref=below,
            send_sem=z_send.at[1],
            recv_sem=z_recv.at[1],
            device_id={"sector": sector + 1},
            device_id_type=MESH,
        )

    def gather_copy(mask, part, block):
        hop = last_hops(mask)[part]
        piece = history.at[block, pl.ds(part * half, half)]
        return pltpu.make_async_remote_copy(
            src_ref=piece,
            dst_ref=piece,
            send_sem=gather_send.at[mask, part],
            recv_sem=gather_recv.at[mask, part],
            device_id={"tm": flipped(me, hop)},
            device_id_type=MESH,
        )

    def gather_start(mask, part):
        hop = last_hops(mask)[part]
        gather_copy(mask, part, flipped(me, mask ^ hop)).start()

    @pl.when(has_below)
    def _():
        down_copy().start()

    singles = [1 << i for i in range(1, times.bit_length() - 1)]
    order = {mask: ((1, 0) if i % 2 == 0 else (0, 1)) for i, mask in enumerate(singles)}
    for turn in range(2):
        for mask in singles:
            gather_start(mask, order[mask][turn])
    for part in range(2):
        gather_start(1, part)

    operator = operator_ref[0]
    raised = jnp.dot(operator, history[me], preferred_element_type=jnp.float32).astype(jnp.bfloat16)
    upward[...] = lax.dot_general(
        raised, operator, (((1,), (1,)), ((), ())), preferred_element_type=jnp.float32
    ).astype(jnp.bfloat16)

    @pl.when(has_above)
    def _():
        up_copy().start()

    turned[...] = operator_ref[0].T

    arrived = set()
    started = {(mask, part) for mask in singles for part in range(2)} | {(1, 0), (1, 1)}

    def gather_arrive(mask, part):
        if (mask, part) in arrived:
            return
        arrived.add((mask, part))
        gather_copy(mask, part, flipped(me, mask)).wait_recv()
        for later in range(2, times):
            if (later, part) not in started and later ^ last_hops(later)[part] == mask:
                started.add((later, part))
                gather_start(later, part)

    for turn in range(2):
        for mask in singles:
            gather_arrive(mask, order[mask][turn])

    @pl.when(has_above)
    def _():
        pltpu.make_async_remote_copy(
            src_ref=above,
            dst_ref=above,
            send_sem=z_send.at[0],
            recv_sem=z_recv.at[0],
            device_id={"sector": sector + 1},
            device_id_type=MESH,
        ).wait_recv()

    @pl.when(sector == sectors - 1)
    def _():
        above[...] = jnp.zeros_like(above)

    lowered = jnp.dot(turned[...], above[...], preferred_element_type=jnp.float32).astype(jnp.bfloat16)
    downward = jnp.dot(lowered, operator_ref[0], preferred_element_type=jnp.float32)

    @pl.when(has_below)
    def _():
        pltpu.make_async_remote_copy(
            src_ref=below,
            dst_ref=below,
            send_sem=z_send.at[1],
            recv_sem=z_recv.at[1],
            device_id={"sector": sector - 1},
            device_id_type=MESH,
        ).wait_recv()

    @pl.when(sector == 0)
    def _():
        below[...] = jnp.zeros_like(below)

    combined = particle_ref[0] * below[...].astype(jnp.float32) + hole_ref[0] * downward
    energy_out[...] = jnp.where(live, combined, jnp.zeros((), jnp.float32)).astype(jnp.bfloat16)

    def row_block(index):
        return pl.ds(pl.multiple_of(index * rows, rows), rows)

    def rows_copy(peer, target, source):
        return pltpu.make_async_remote_copy(
            src_ref=energy_out.at[row_block(target)],
            dst_ref=energy_in.at[row_block(source)],
            send_sem=rows_send.at[peer],
            recv_sem=rows_recv.at[peer],
            device_id={"tm": flipped(me, peer)},
            device_id_type=MESH,
        )

    for mask in reversed(range(1, times)):
        rows_copy(mask, flipped(me, mask), me).start()
    energy_in[row_block(me)] = energy_out[row_block(me)]

    for mask in range(2, times, 2):
        for part in range(2):
            gather_arrive(mask, part)
    for mask in range(1, times, 2):
        for part in range(2):
            gather_arrive(mask, part)
    for mask in range(1, times):
        rows_copy(mask, flipped(me, mask), flipped(me, mask)).wait_recv()

    row_ids = me * rows + lax.broadcasted_iota(jnp.int32, (rows, states), 0)
    column_ids = lax.broadcasted_iota(jnp.int32, (rows, states), 1)
    on_diagonal = row_ids == column_ids
    rates = jnp.sum(
        jnp.where(on_diagonal, energy_ref[...], jnp.zeros((), jnp.float32)), axis=1, keepdims=True
    )
    decay = jnp.exp(-step_size * rates)
    shown = on_diagonal & (row_ids < size)

    def out_copy(moment, place):
        return pltpu.make_async_remote_copy(
            src_ref=fresh.at[moment],
            dst_ref=out_ref.at[0, 0, row_block(place)],
            send_sem=out_send.at[moment],
            recv_sem=out_recv.at[place],
            device_id={"tm": moment},
            device_id_type=MESH,
        )

    running = jnp.zeros((rows, states), jnp.float32)
    for moment in range(times):
        depth = (times - moment) * rows
        product = jnp.dot(
            energy_in[0:depth], history[moment], preferred_element_type=jnp.float32
        )
        if moment == 0:
            sums[...] = product
        else:
            sums[moment * rows : states] += product
        running = decay * running + step_size * sums[moment * rows : (moment + 1) * rows]
        free_part = jnp.where(
            shown, jnp.exp(-rates * (moment * step_size)), jnp.zeros((), jnp.float32)
        )
        fresh[moment] = (free_part - step_size * running).astype(jnp.bfloat16)

        @pl.when(me != moment)
        def _():
            out_copy(moment, me).start()

        @pl.when(me == moment)
        def _():
            out_ref[0, 0, row_block(me)] = fresh[moment]

    for mask in range(1, times):
        pltpu.make_async_remote_copy(
            src_ref=fresh.at[0],
            dst_ref=out_ref.at[0, 0, row_block(flipped(me, mask))],
            send_sem=out_send.at[0],
            recv_sem=out_recv.at[flipped(me, mask)],
            device_id={"tm": flipped(me, mask)},
            device_id_type=MESH,
        ).wait_recv()
    for moment in range(times):

        @pl.when(me != moment)
        def _():
            out_copy(moment, me).wait_send()

    for mask in range(1, times):
        rows_copy(mask, flipped(me, mask), me).wait_send()
        for part in range(2):
            gather_copy(mask, part, flipped(me, mask)).wait_send()

    @pl.when(has_below)
    def _():
        down_copy().wait_send()

    @pl.when(has_above)
    def _():
        up_copy().wait_send()


def fused_device(propagator, rising_op, energies, hyb_particle, hyb_hole, sector_sizes):
    times = lax.axis_size("tm")
    states = propagator.shape[-1]
    square = (states, states)
    narrow, wide = jnp.bfloat16, jnp.float32
    vmem = pl.BlockSpec(memory_space=pltpu.VMEM)
    smem = pl.BlockSpec(memory_space=pltpu.SMEM)
    dma = pltpu.SemaphoreType.DMA
    return pl.pallas_call(
        functools.partial(fused_kernel, times, lax.axis_size("sector")),
        out_shape=jax.ShapeDtypeStruct(propagator.shape, narrow),
        in_specs=[smem, smem, smem, vmem, vmem, vmem],
        out_specs=vmem,
        scratch_shapes=[
            pltpu.VMEM((times,) + square, narrow),
            pltpu.VMEM(square, narrow),
            pltpu.VMEM(square, narrow),
            pltpu.VMEM(square, narrow),
            pltpu.VMEM(square, narrow),
            pltpu.VMEM(square, narrow),
            pltpu.VMEM(square, narrow),
            pltpu.VMEM(square, wide),
            pltpu.VMEM((times, states // times, states), narrow),
            dma((2,)),
            dma((2,)),
            dma((times, 2)),
            dma((times, 2)),
            dma((times,)),
            dma((times,)),
            dma((times,)),
            dma((times,)),
        ],
        compiler_params=pltpu.CompilerParams(
            collective_id=0, has_side_effects=True, vmem_limit_bytes=60 * 2**20
        ),
    )(sector_sizes, hyb_particle, hyb_hole, propagator, rising_op, energies)


def per_device(propagator, rising_op, energies, hyb_particle, hyb_hole, sector_sizes):
    times = lax.axis_size("tm")
    states = propagator.shape[-1]
    fits = (
        propagator.shape[1] == 1
        and times > 2
        and times & (times - 1) == 0
        and states % (times * ROW_TILE) == 0
        and states % (2 * ROW_TILE) == 0
        and states % LANES == 0
    )
    chosen = fused_device if fits else general_device
    return chosen(propagator, rising_op, energies, hyb_particle, hyb_hole, sector_sizes)


def solution(mesh):
    placed = (
        P("sector", "tm", None, None),
        P("sector", None, None),
        P("sector", None),
        P("tm"),
        P("tm"),
        P("sector"),
    )
    return jax.shard_map(
        per_device,
        mesh=mesh,
        in_specs=placed,
        out_specs=P("sector", "tm", None, None),
        check_vma=False,
    )
```

```python
import functools
import jax
import jax.numpy as jnp
from jax import lax
from jax.experimental import pallas as pl
from jax.experimental.pallas import tpu as pltpu
from jax.sharding import PartitionSpec as P


def shifted(block, axis, distance):
    devices = range(lax.axis_size(axis))
    route = [(i - distance, i) for i in devices if i - distance in devices]
    return lax.ppermute(block, axis, route)


def general_device(propagator, rising_op, energies, hyb_particle, hyb_hole, sector_sizes):
    t_dev = propagator.shape[1]
    states = propagator.shape[2]
    time_count = t_dev * lax.axis_size("tm")
    step_size = 1.0 / time_count
    positions = jnp.arange(states, dtype=jnp.int32)
    live_mask = positions < sector_sizes[0]
    square = live_mask[:, None] & live_mask[None, :]
    masked_prop = jnp.where(square[None], propagator[0], jnp.zeros((), jnp.bfloat16))
    operator = rising_op[0]
    raised = jnp.einsum(
        "ik,tkl->til", operator, masked_prop, preferred_element_type=jnp.float32
    ).astype(jnp.bfloat16)
    upward = jnp.einsum("tik,jk->tij", raised, operator, preferred_element_type=jnp.float32).astype(
        jnp.bfloat16
    )
    from_below = shifted(upward, "sector", 1)
    from_above = shifted(masked_prop, "sector", -1)
    lowered = jnp.einsum(
        "ki,tkl->til", operator, from_above, preferred_element_type=jnp.float32
    ).astype(jnp.bfloat16)
    downward = jnp.einsum("tik,kl->til", lowered, operator, preferred_element_type=jnp.float32)
    combined = (
        hyb_particle[:, None, None] * from_below.astype(jnp.float32)
        + hyb_hole[:, None, None] * downward
    )
    self_energy = jnp.where(square[None], combined, jnp.zeros((), jnp.float32)).astype(jnp.bfloat16)
    rows_each = states // lax.axis_size("tm")
    first_row = lax.axis_index("tm") * rows_each
    lag_rows = lax.all_to_all(self_energy, "tm", split_axis=1, concat_axis=0, tiled=True)
    history = lax.all_gather(masked_prop, "tm", axis=0, tiled=True)
    mirrored = jnp.concatenate([history[::-1], history], 0)
    slots = jnp.arange(time_count, dtype=jnp.int32)
    wide_slots = jnp.arange(time_count + 1, dtype=jnp.int32)

    def pair_step(lag, sums):
        forward, backward = sums
        other = time_count - 1 - lag
        window = lax.dynamic_slice_in_dim(mirrored, lag, time_count + 1, 0)
        near = lax.dynamic_index_in_dim(lag_rows, lag, 0, keepdims=False)
        far = lax.dynamic_index_in_dim(lag_rows, other, 0, keepdims=False)
        left = jnp.where((wide_slots < time_count - lag)[:, None, None], near[None], far[None])
        product = jnp.einsum("uik,ukl->uil", left, window, preferred_element_type=jnp.float32)
        backward = backward + jnp.where(
            (slots < time_count - lag)[:, None, None],
            product[:time_count],
            jnp.zeros((), jnp.float32),
        )
        forward = forward + jnp.where(
            (slots >= time_count - lag - 1)[:, None, None], product[1:], jnp.zeros((), jnp.float32)
        )
        return (forward, backward)

    empty_rows = jnp.zeros((time_count, rows_each, states), jnp.float32)
    forward, backward = lax.fori_loop(0, time_count // 2, pair_step, (empty_rows, empty_rows))
    convolved = step_size * (forward + backward[::-1])
    row_ids = first_row + jnp.arange(rows_each, dtype=jnp.int32)
    row_rates = lax.dynamic_slice_in_dim(energies[0], first_row, rows_each, 0)
    decay_rows = jnp.exp(-step_size * row_rates)

    def advance(running, term):
        running = decay_rows[:, None] * running + term
        return (running, running)

    _, summed = lax.scan(advance, jnp.zeros((rows_each, states), jnp.float32), convolved)
    moments = jnp.arange(time_count).astype(jnp.float32) * step_size
    live_rows = row_ids < sector_sizes[0]
    free_part = jnp.where(
        live_rows[None, :],
        jnp.exp(-row_rates[None, :] * moments[:, None]),
        jnp.zeros((), jnp.float32),
    )
    diagonal = jnp.where(
        (row_ids[:, None] == positions[None, :])[None],
        free_part[:, :, None],
        jnp.zeros((), jnp.float32),
    )
    new_rows = (diagonal - step_size * summed).astype(jnp.bfloat16)
    return lax.all_to_all(new_rows, "tm", split_axis=0, concat_axis=1, tiled=True)[None]


MESH = pl.DeviceIdType.MESH
ROW_TILE = 16
LANES = 128
SUBLANES = 8
PARTS = 4


def flipped(index, mask):
    bit = 1
    while bit <= mask:
        if mask & bit:
            index = index + bit - 2 * bit * lax.rem(lax.div(index, bit), 2)
        bit *= 2
    return index


def last_hop(mask, part):
    bits = [1 << i for i in range(mask.bit_length()) if mask >> i & 1]
    if bits[0] == 1:
        return 1
    return bits[0] if part < PARTS // 2 else bits[-1]


def fused_kernel(
    times,
    sectors,
    size_ref,
    particle_ref,
    hole_ref,
    prop_ref,
    operator_ref,
    energy_ref,
    out_ref,
    history,
    lower_operator,
    turned,
    pair,
    up_rows,
    down_rows,
    below,
    above,
    energy_in,
    sums,
    fresh,
    strengths,
    operator_send,
    operator_recv,
    up_send,
    up_recv,
    down_send,
    down_recv,
    gather_send,
    gather_recv,
    strength_send,
    strength_recv,
    out_send,
    out_recv,
):
    states = prop_ref.shape[-1]
    rows = states // times
    half = states // 2
    piece_rows = states // PARTS
    step_size = 1.0 / times
    me = lax.axis_index("tm")
    sector = lax.axis_index("sector")
    has_below = sector > 0
    has_above = sector < sectors - 1

    barrier = pltpu.get_barrier_semaphore()
    for mask in range(1, times):
        pl.semaphore_signal(
            barrier, inc=1, device_id={"tm": flipped(me, mask)}, device_id_type=MESH
        )

    @pl.when(has_below)
    def _():
        pl.semaphore_signal(barrier, inc=1, device_id={"sector": sector - 1}, device_id_type=MESH)

    @pl.when(has_above)
    def _():
        pl.semaphore_signal(barrier, inc=1, device_id={"sector": sector + 1}, device_id_type=MESH)

    size = size_ref[0]
    live = (lax.broadcasted_iota(jnp.int32, (states, states), 0) < size) & (
        lax.broadcasted_iota(jnp.int32, (states, states), 1) < size
    )
    history[me] = jnp.where(
        live, prop_ref[0, 0].astype(jnp.float32), jnp.zeros((), jnp.float32)
    ).astype(jnp.bfloat16)
    first_line = lax.broadcasted_iota(jnp.int32, strengths.shape[1:], 0) == 0
    strengths[me] = jnp.where(first_line, particle_ref[0], hole_ref[0])

    neighbours = jnp.where(has_below, 1, 0) + jnp.where(has_above, 1, 0)
    pl.semaphore_wait(barrier, times - 1 + neighbours)

    def row_block(index):
        return pl.ds(pl.multiple_of(index * rows, rows), rows)

    def half_block(index):
        return pl.ds(pl.multiple_of(index * half, half), half)

    my_half = lax.rem(me, 2)

    def operator_copy():
        return pltpu.make_async_remote_copy(
            src_ref=operator_ref.at[0, half_block(my_half)],
            dst_ref=lower_operator.at[half_block(my_half)],
            send_sem=operator_send.at[0],
            recv_sem=operator_recv.at[0],
            device_id={"sector": sector + 1},
            device_id_type=MESH,
        )

    def share_copy(which):
        return pltpu.make_async_remote_copy(
            src_ref=lower_operator.at[half_block(which)],
            dst_ref=lower_operator.at[half_block(which)],
            send_sem=operator_send.at[1],
            recv_sem=operator_recv.at[1],
            device_id={"tm": flipped(me, 1)},
            device_id_type=MESH,
        )

    def up_copy(mask, step=1):
        block = row_block(flipped(me, mask))
        return pltpu.make_async_remote_copy(
            src_ref=up_rows.at[block],
            dst_ref=below.at[block],
            send_sem=up_send.at[mask],
            recv_sem=up_recv.at[mask],
            device_id={"sector": sector + step},
            device_id_type=MESH,
        )

    def down_copy(mask, step=-1):
        block = row_block(flipped(me, mask))
        return pltpu.make_async_remote_copy(
            src_ref=down_rows.at[block],
            dst_ref=above.at[block],
            send_sem=down_send.at[mask],
            recv_sem=down_recv.at[mask],
            device_id={"sector": sector + step},
            device_id_type=MESH,
        )

    def gather_copy(mask, part, block):
        piece = history.at[block, pl.ds(part * piece_rows, piece_rows)]
        return pltpu.make_async_remote_copy(
            src_ref=piece,
            dst_ref=piece,
            send_sem=gather_send.at[mask, part],
            recv_sem=gather_recv.at[mask, part],
            device_id={"tm": flipped(me, last_hop(mask, part))},
            device_id_type=MESH,
        )

    def strength_copy(mask, block):
        return pltpu.make_async_remote_copy(
            src_ref=strengths.at[block],
            dst_ref=strengths.at[block],
            send_sem=strength_send.at[mask],
            recv_sem=strength_recv.at[mask],
            device_id={"tm": flipped(me, mask)},
            device_id_type=MESH,
        )

    def gather_start(mask, part):
        gather_copy(mask, part, flipped(me, mask ^ last_hop(mask, part))).start()

    forward = list(range(PARTS))
    backward = forward[PARTS // 2 :] + forward[: PARTS // 2]
    mixed = [p for pair_of in zip(forward, backward) for p in pair_of][:PARTS]
    singles = [1 << i for i in range(1, times.bit_length() - 1)]
    order = {mask: (backward if i % 2 == 0 else forward) for i, mask in enumerate(singles)}
    started = {(mask, part) for mask in [1] + singles for part in range(PARTS)}
    arrived = set()
    for turn in range(PARTS):
        for mask in singles:
            gather_start(mask, order[mask][turn])
        gather_start(1, turn)

    @pl.when(has_above)
    def _():
        operator_copy().start()

    for mask in range(1, times):
        strength_copy(mask, me).start()

    def gather_arrive(mask, part):
        if (mask, part) in arrived:
            return
        arrived.add((mask, part))
        gather_copy(mask, part, flipped(me, mask)).wait_recv()
        for later in range(2, times):
            if (later, part) not in started and later ^ last_hop(later, part) == mask:
                started.add((later, part))
                gather_start(later, part)

    def send_up(mask, raised):
        up_rows[row_block(flipped(me, mask))] = lax.dot_general(
            raised, operator_ref[0], (((1,), (1,)), ((), ())), preferred_element_type=jnp.float32
        ).astype(jnp.bfloat16)

        @pl.when(has_above)
        def _():
            up_copy(mask).start()

    def send_down(mask, lowered):
        down_rows[row_block(flipped(me, mask))] = jnp.dot(
            lowered, lower_operator[...], preferred_element_type=jnp.float32
        ).astype(jnp.bfloat16)

        @pl.when(has_below)
        def _():
            down_copy(mask).start()

    def product_of(left, mask):
        return jnp.dot(
            left, history[flipped(me, mask)], preferred_element_type=jnp.float32
        ).astype(jnp.bfloat16)

    pair[0:rows] = operator_ref[0, row_block(me)]
    send_up(0, product_of(pair[0:rows], 0))
    for part in range(PARTS):
        gather_arrive(1, part)
    send_up(1, product_of(pair[0:rows], 1))
    for turn in range(PARTS // 2):
        for mask in singles:
            gather_arrive(mask, order[mask][turn])

    @pl.when(has_below)
    def _():
        pltpu.make_async_remote_copy(
            src_ref=lower_operator.at[half_block(my_half)],
            dst_ref=lower_operator.at[half_block(my_half)],
            send_sem=operator_send.at[0],
            recv_sem=operator_recv.at[0],
            device_id={"sector": sector - 1},
            device_id_type=MESH,
        ).wait_recv()
        share_copy(my_half).start()
        share_copy(1 - my_half).wait_recv()

    @pl.when(sector == 0)
    def _():
        lower_operator[...] = jnp.zeros_like(lower_operator)

    turned[...] = lower_operator[...].T
    pair[rows : 2 * rows] = turned[row_block(me)]
    for mask in range(2):
        send_down(mask, product_of(pair[rows : 2 * rows], mask))

    for turn in range(PARTS // 2, PARTS):
        for mask in singles:
            gather_arrive(mask, order[mask][turn])

    ranked = sorted(range(2, times), key=lambda m: (bin(m >> 1).count("1"), m & 1, m))
    for mask in ranked:
        for part in mixed:
            gather_arrive(mask, part)
        both = product_of(pair[...], mask)
        send_up(mask, both[0:rows])
        send_down(mask, both[rows : 2 * rows])

    @pl.when(sector == 0)
    def _():
        below[...] = jnp.zeros_like(below)

    @pl.when(sector == sectors - 1)
    def _():
        above[...] = jnp.zeros_like(above)

    row_ids = me * rows + lax.broadcasted_iota(jnp.int32, (rows, states), 0)
    column_ids = lax.broadcasted_iota(jnp.int32, (rows, states), 1)
    on_diagonal = row_ids == column_ids
    rates = jnp.sum(
        jnp.where(on_diagonal, energy_ref[...], jnp.zeros((), jnp.float32)), axis=1, keepdims=True
    )
    decay = jnp.exp(-step_size * rates)
    shown = on_diagonal & (row_ids < size)
    live_rows = (row_ids < size) & (column_ids < size)

    for mask in range(1, times):
        strength_copy(mask, flipped(me, mask)).wait_recv()

    @pl.when(has_below)
    def _():
        for mask in range(times):
            up_copy(mask, -1).wait_recv()

    @pl.when(has_above)
    def _():
        for mask in range(times):
            down_copy(mask, 1).wait_recv()

    for moment in range(times):
        place = pl.ds(moment * rows, rows)
        combined = strengths[moment, 0:1, 0:1] * below[place].astype(jnp.float32) + strengths[
            moment, 1:2, 0:1
        ] * above[place].astype(jnp.float32)
        energy_in[place] = jnp.where(live_rows, combined, jnp.zeros((), jnp.float32)).astype(
            jnp.bfloat16
        )

    def out_copy(moment, place):
        return pltpu.make_async_remote_copy(
            src_ref=fresh.at[moment],
            dst_ref=out_ref.at[0, 0, row_block(place)],
            send_sem=out_send.at[moment],
            recv_sem=out_recv.at[place],
            device_id={"tm": moment},
            device_id_type=MESH,
        )

    running = jnp.zeros((rows, states), jnp.float32)
    for moment in range(times):
        depth = (times - moment) * rows
        product = jnp.dot(
            energy_in[0:depth], history[moment], preferred_element_type=jnp.float32
        )
        if moment == 0:
            sums[...] = product
        else:
            sums[moment * rows : states] += product
        running = decay * running + step_size * sums[moment * rows : (moment + 1) * rows]
        free_part = jnp.where(
            shown, jnp.exp(-rates * (moment * step_size)), jnp.zeros((), jnp.float32)
        )
        fresh[moment] = (free_part - step_size * running).astype(jnp.bfloat16)

        @pl.when(me != moment)
        def _():
            out_copy(moment, me).start()

        @pl.when(me == moment)
        def _():
            out_ref[0, 0, row_block(me)] = fresh[moment]

    for mask in range(1, times):
        pltpu.make_async_remote_copy(
            src_ref=fresh.at[0],
            dst_ref=out_ref.at[0, 0, row_block(flipped(me, mask))],
            send_sem=out_send.at[0],
            recv_sem=out_recv.at[flipped(me, mask)],
            device_id={"tm": flipped(me, mask)},
            device_id_type=MESH,
        ).wait_recv()
    for moment in range(times):

        @pl.when(me != moment)
        def _():
            out_copy(moment, me).wait_send()

    for mask in range(1, times):
        strength_copy(mask, me).wait_send()
        for part in range(PARTS):
            gather_copy(mask, part, flipped(me, mask)).wait_send()

    @pl.when(has_below)
    def _():
        share_copy(my_half).wait_send()
        for mask in range(times):
            down_copy(mask).wait_send()

    @pl.when(has_above)
    def _():
        operator_copy().wait_send()
        for mask in range(times):
            up_copy(mask).wait_send()


def fused_device(propagator, rising_op, energies, hyb_particle, hyb_hole, sector_sizes):
    times = lax.axis_size("tm")
    states = propagator.shape[-1]
    square = (states, states)
    narrow, wide = jnp.bfloat16, jnp.float32
    vmem = pl.BlockSpec(memory_space=pltpu.VMEM)
    smem = pl.BlockSpec(memory_space=pltpu.SMEM)
    dma = pltpu.SemaphoreType.DMA
    return pl.pallas_call(
        functools.partial(fused_kernel, times, lax.axis_size("sector")),
        out_shape=jax.ShapeDtypeStruct(propagator.shape, narrow),
        in_specs=[smem, smem, smem, vmem, vmem, vmem],
        out_specs=vmem,
        scratch_shapes=[
            pltpu.VMEM((times,) + square, narrow),
            pltpu.VMEM(square, narrow),
            pltpu.VMEM(square, narrow),
            pltpu.VMEM((2 * (states // times), states), narrow),
            pltpu.VMEM(square, narrow),
            pltpu.VMEM(square, narrow),
            pltpu.VMEM(square, narrow),
            pltpu.VMEM(square, narrow),
            pltpu.VMEM(square, narrow),
            pltpu.VMEM(square, wide),
            pltpu.VMEM((times, states // times, states), narrow),
            pltpu.VMEM((times, SUBLANES, LANES), wide),
            dma((2,)),
            dma((2,)),
            dma((times,)),
            dma((times,)),
            dma((times,)),
            dma((times,)),
            dma((times, PARTS)),
            dma((times, PARTS)),
            dma((times,)),
            dma((times,)),
            dma((times,)),
            dma((times,)),
        ],
        compiler_params=pltpu.CompilerParams(
            collective_id=0, has_side_effects=True, vmem_limit_bytes=60 * 2**20
        ),
    )(sector_sizes, hyb_particle, hyb_hole, propagator, rising_op, energies)


def per_device(propagator, rising_op, energies, hyb_particle, hyb_hole, sector_sizes):
    times = lax.axis_size("tm")
    states = propagator.shape[-1]
    fits = (
        propagator.shape[1] == 1
        and times > 2
        and times & (times - 1) == 0
        and states % (times * ROW_TILE) == 0
        and states % (PARTS * ROW_TILE) == 0
        and states % LANES == 0
    )
    chosen = fused_device if fits else general_device
    return chosen(propagator, rising_op, energies, hyb_particle, hyb_hole, sector_sizes)


def solution(mesh):
    placed = (
        P("sector", "tm", None, None),
        P("sector", None, None),
        P("sector", None),
        P("tm"),
        P("tm"),
        P("sector"),
    )
    return jax.shard_map(
        per_device,
        mesh=mesh,
        in_specs=placed,
        out_specs=P("sector", "tm", None, None),
        check_vma=False,
    )
```

```python
import functools
import jax
import jax.numpy as jnp
from jax import lax
from jax.experimental import pallas as pl
from jax.experimental.pallas import tpu as pltpu
from jax.sharding import PartitionSpec as P


def shifted(block, axis, distance):
    devices = range(lax.axis_size(axis))
    route = [(i - distance, i) for i in devices if i - distance in devices]
    return lax.ppermute(block, axis, route)


def general_device(propagator, rising_op, energies, hyb_particle, hyb_hole, sector_sizes):
    t_dev = propagator.shape[1]
    states = propagator.shape[2]
    time_count = t_dev * lax.axis_size("tm")
    step_size = 1.0 / time_count
    positions = jnp.arange(states, dtype=jnp.int32)
    live_mask = positions < sector_sizes[0]
    square = live_mask[:, None] & live_mask[None, :]
    masked_prop = jnp.where(square[None], propagator[0], jnp.zeros((), jnp.bfloat16))
    operator = rising_op[0]
    raised = jnp.einsum(
        "ik,tkl->til", operator, masked_prop, preferred_element_type=jnp.float32
    ).astype(jnp.bfloat16)
    upward = jnp.einsum("tik,jk->tij", raised, operator, preferred_element_type=jnp.float32).astype(
        jnp.bfloat16
    )
    from_below = shifted(upward, "sector", 1)
    from_above = shifted(masked_prop, "sector", -1)
    lowered = jnp.einsum(
        "ki,tkl->til", operator, from_above, preferred_element_type=jnp.float32
    ).astype(jnp.bfloat16)
    downward = jnp.einsum("tik,kl->til", lowered, operator, preferred_element_type=jnp.float32)
    combined = (
        hyb_particle[:, None, None] * from_below.astype(jnp.float32)
        + hyb_hole[:, None, None] * downward
    )
    self_energy = jnp.where(square[None], combined, jnp.zeros((), jnp.float32)).astype(jnp.bfloat16)
    rows_each = states // lax.axis_size("tm")
    first_row = lax.axis_index("tm") * rows_each
    lag_rows = lax.all_to_all(self_energy, "tm", split_axis=1, concat_axis=0, tiled=True)
    history = lax.all_gather(masked_prop, "tm", axis=0, tiled=True)
    mirrored = jnp.concatenate([history[::-1], history], 0)
    slots = jnp.arange(time_count, dtype=jnp.int32)
    wide_slots = jnp.arange(time_count + 1, dtype=jnp.int32)

    def pair_step(lag, sums):
        forward, backward = sums
        other = time_count - 1 - lag
        window = lax.dynamic_slice_in_dim(mirrored, lag, time_count + 1, 0)
        near = lax.dynamic_index_in_dim(lag_rows, lag, 0, keepdims=False)
        far = lax.dynamic_index_in_dim(lag_rows, other, 0, keepdims=False)
        left = jnp.where((wide_slots < time_count - lag)[:, None, None], near[None], far[None])
        product = jnp.einsum("uik,ukl->uil", left, window, preferred_element_type=jnp.float32)
        backward = backward + jnp.where(
            (slots < time_count - lag)[:, None, None],
            product[:time_count],
            jnp.zeros((), jnp.float32),
        )
        forward = forward + jnp.where(
            (slots >= time_count - lag - 1)[:, None, None], product[1:], jnp.zeros((), jnp.float32)
        )
        return (forward, backward)

    empty_rows = jnp.zeros((time_count, rows_each, states), jnp.float32)
    forward, backward = lax.fori_loop(0, time_count // 2, pair_step, (empty_rows, empty_rows))
    convolved = step_size * (forward + backward[::-1])
    row_ids = first_row + jnp.arange(rows_each, dtype=jnp.int32)
    row_rates = lax.dynamic_slice_in_dim(energies[0], first_row, rows_each, 0)
    decay_rows = jnp.exp(-step_size * row_rates)

    def advance(running, term):
        running = decay_rows[:, None] * running + term
        return (running, running)

    _, summed = lax.scan(advance, jnp.zeros((rows_each, states), jnp.float32), convolved)
    moments = jnp.arange(time_count).astype(jnp.float32) * step_size
    live_rows = row_ids < sector_sizes[0]
    free_part = jnp.where(
        live_rows[None, :],
        jnp.exp(-row_rates[None, :] * moments[:, None]),
        jnp.zeros((), jnp.float32),
    )
    diagonal = jnp.where(
        (row_ids[:, None] == positions[None, :])[None],
        free_part[:, :, None],
        jnp.zeros((), jnp.float32),
    )
    new_rows = (diagonal - step_size * summed).astype(jnp.bfloat16)
    return lax.all_to_all(new_rows, "tm", split_axis=0, concat_axis=1, tiled=True)[None]


MESH = pl.DeviceIdType.MESH
ROW_TILE = 16
LANES = 128
SUBLANES = 8
PARTS = 4


def flipped(index, mask):
    bit = 1
    while bit <= mask:
        if mask & bit:
            index = index + bit - 2 * bit * lax.rem(lax.div(index, bit), 2)
        bit *= 2
    return index


def last_hop(mask, part):
    bits = [1 << i for i in range(mask.bit_length()) if mask >> i & 1]
    if bits[0] == 1:
        return 1
    return bits[0] if part < PARTS // 2 else bits[-1]


def fused_kernel(
    times,
    sectors,
    size_ref,
    particle_ref,
    hole_ref,
    prop_ref,
    operator_ref,
    energy_ref,
    out_ref,
    history,
    lower_operator,
    turned,
    pair,
    up_rows,
    down_rows,
    below,
    above,
    energy_in,
    sums,
    fresh,
    strengths,
    operator_send,
    operator_recv,
    up_send,
    up_recv,
    down_send,
    down_recv,
    gather_send,
    gather_recv,
    strength_send,
    strength_recv,
    out_send,
    out_recv,
):
    states = prop_ref.shape[-1]
    rows = states // times
    half = states // 2
    piece_rows = states // PARTS
    step_size = 1.0 / times
    me = lax.axis_index("tm")
    sector = lax.axis_index("sector")
    has_below = sector > 0
    has_above = sector < sectors - 1

    barrier = pltpu.get_barrier_semaphore()
    for mask in range(1, times):
        pl.semaphore_signal(
            barrier, inc=1, device_id={"tm": flipped(me, mask)}, device_id_type=MESH
        )

    @pl.when(has_below)
    def _():
        pl.semaphore_signal(barrier, inc=1, device_id={"sector": sector - 1}, device_id_type=MESH)

    @pl.when(has_above)
    def _():
        pl.semaphore_signal(barrier, inc=1, device_id={"sector": sector + 1}, device_id_type=MESH)

    size = size_ref[0]
    live = (lax.broadcasted_iota(jnp.int32, (states, states), 0) < size) & (
        lax.broadcasted_iota(jnp.int32, (states, states), 1) < size
    )
    history[me] = jnp.where(
        live, prop_ref[0, 0].astype(jnp.float32), jnp.zeros((), jnp.float32)
    ).astype(jnp.bfloat16)
    first_line = lax.broadcasted_iota(jnp.int32, strengths.shape[1:], 0) == 0
    strengths[me] = jnp.where(first_line, particle_ref[0], hole_ref[0])

    neighbours = jnp.where(has_below, 1, 0) + jnp.where(has_above, 1, 0)
    pl.semaphore_wait(barrier, times - 1 + neighbours)

    def row_block(index):
        return pl.ds(pl.multiple_of(index * rows, rows), rows)

    def half_block(index):
        return pl.ds(pl.multiple_of(index * half, half), half)

    my_half = lax.rem(me, 2)

    def operator_copy():
        return pltpu.make_async_remote_copy(
            src_ref=operator_ref.at[0, half_block(my_half)],
            dst_ref=lower_operator.at[half_block(my_half)],
            send_sem=operator_send.at[0],
            recv_sem=operator_recv.at[0],
            device_id={"sector": sector + 1},
            device_id_type=MESH,
        )

    def share_copy(which):
        return pltpu.make_async_remote_copy(
            src_ref=lower_operator.at[half_block(which)],
            dst_ref=lower_operator.at[half_block(which)],
            send_sem=operator_send.at[1],
            recv_sem=operator_recv.at[1],
            device_id={"tm": flipped(me, 1)},
            device_id_type=MESH,
        )

    def up_copy(mask, step=1):
        block = row_block(flipped(me, mask))
        return pltpu.make_async_remote_copy(
            src_ref=up_rows.at[block],
            dst_ref=below.at[block],
            send_sem=up_send.at[mask],
            recv_sem=up_recv.at[mask],
            device_id={"sector": sector + step},
            device_id_type=MESH,
        )

    def down_copy(mask, step=-1):
        block = row_block(flipped(me, mask))
        return pltpu.make_async_remote_copy(
            src_ref=down_rows.at[block],
            dst_ref=above.at[block],
            send_sem=down_send.at[mask],
            recv_sem=down_recv.at[mask],
            device_id={"sector": sector + step},
            device_id_type=MESH,
        )

    def gather_copy(mask, part, block):
        piece = history.at[block, pl.ds(part * piece_rows, piece_rows)]
        return pltpu.make_async_remote_copy(
            src_ref=piece,
            dst_ref=piece,
            send_sem=gather_send.at[mask, part],
            recv_sem=gather_recv.at[mask, part],
            device_id={"tm": flipped(me, last_hop(mask, part))},
            device_id_type=MESH,
        )

    def strength_copy(mask, block):
        return pltpu.make_async_remote_copy(
            src_ref=strengths.at[block],
            dst_ref=strengths.at[block],
            send_sem=strength_send.at[mask],
            recv_sem=strength_recv.at[mask],
            device_id={"tm": flipped(me, mask)},
            device_id_type=MESH,
        )

    def gather_start(mask, part):
        gather_copy(mask, part, flipped(me, mask ^ last_hop(mask, part))).start()

    forward = list(range(PARTS))
    backward = forward[PARTS // 2 :] + forward[: PARTS // 2]
    mixed = [p for pair_of in zip(forward, backward) for p in pair_of][:PARTS]
    singles = [1 << i for i in range(1, times.bit_length() - 1)]
    order = {mask: (backward if i % 2 == 0 else forward) for i, mask in enumerate(singles)}
    started = {(mask, part) for mask in [1] + singles for part in range(PARTS)}
    arrived = set()
    for turn in range(PARTS):
        for mask in singles:
            gather_start(mask, order[mask][turn])
        gather_start(1, turn)

    @pl.when(has_above)
    def _():
        operator_copy().start()

    for mask in range(1, times):
        strength_copy(mask, me).start()

    def gather_arrive(mask, part):
        if (mask, part) in arrived:
            return
        arrived.add((mask, part))
        gather_copy(mask, part, flipped(me, mask)).wait_recv()
        for later in range(2, times):
            if (later, part) not in started and later ^ last_hop(later, part) == mask:
                started.add((later, part))
                gather_start(later, part)

    def send_up(mask, raised):
        up_rows[row_block(flipped(me, mask))] = lax.dot_general(
            raised, operator_ref[0], (((1,), (1,)), ((), ())), preferred_element_type=jnp.float32
        ).astype(jnp.bfloat16)

        @pl.when(has_above)
        def _():
            up_copy(mask).start()

    def send_down(mask, lowered):
        down_rows[row_block(flipped(me, mask))] = jnp.dot(
            lowered, lower_operator[...], preferred_element_type=jnp.float32
        ).astype(jnp.bfloat16)

        @pl.when(has_below)
        def _():
            down_copy(mask).start()

    def product_of(left, mask):
        return jnp.dot(
            left, history[flipped(me, mask)], preferred_element_type=jnp.float32
        ).astype(jnp.bfloat16)

    pair[0:rows] = operator_ref[0, row_block(me)]
    send_up(0, product_of(pair[0:rows], 0))
    for part in range(PARTS):
        gather_arrive(1, part)
    send_up(1, product_of(pair[0:rows], 1))
    for turn in range(PARTS // 2):
        for mask in singles:
            gather_arrive(mask, order[mask][turn])

    @pl.when(has_below)
    def _():
        pltpu.make_async_remote_copy(
            src_ref=lower_operator.at[half_block(my_half)],
            dst_ref=lower_operator.at[half_block(my_half)],
            send_sem=operator_send.at[0],
            recv_sem=operator_recv.at[0],
            device_id={"sector": sector - 1},
            device_id_type=MESH,
        ).wait_recv()
        share_copy(my_half).start()
        share_copy(1 - my_half).wait_recv()

    @pl.when(sector == 0)
    def _():
        lower_operator[...] = jnp.zeros_like(lower_operator)

    turned[...] = lower_operator[...].T
    pair[rows : 2 * rows] = turned[row_block(me)]
    for mask in range(2):
        send_down(mask, product_of(pair[rows : 2 * rows], mask))

    for turn in range(PARTS // 2, PARTS):
        for mask in singles:
            gather_arrive(mask, order[mask][turn])

    ranked = sorted(range(2, times), key=lambda m: (bin(m >> 1).count("1"), m & 1, m))
    for mask in ranked:
        for part in mixed:
            gather_arrive(mask, part)
        both = product_of(pair[...], mask)
        send_up(mask, both[0:rows])
        send_down(mask, both[rows : 2 * rows])

    @pl.when(sector == 0)
    def _():
        below[...] = jnp.zeros_like(below)

    @pl.when(sector == sectors - 1)
    def _():
        above[...] = jnp.zeros_like(above)

    row_ids = me * rows + lax.broadcasted_iota(jnp.int32, (rows, states), 0)
    column_ids = lax.broadcasted_iota(jnp.int32, (rows, states), 1)
    on_diagonal = row_ids == column_ids
    rates = jnp.sum(
        jnp.where(on_diagonal, energy_ref[...], jnp.zeros((), jnp.float32)), axis=1, keepdims=True
    )
    decay = jnp.exp(-step_size * rates)
    shown = on_diagonal & (row_ids < size)
    live_rows = (row_ids < size) & (column_ids < size)

    for mask in range(1, times):
        strength_copy(mask, flipped(me, mask)).wait_recv()

    @pl.when(has_below)
    def _():
        for mask in range(times):
            up_copy(mask, -1).wait_recv()

    @pl.when(has_above)
    def _():
        for mask in range(times):
            down_copy(mask, 1).wait_recv()

    for moment in range(times):
        place = pl.ds(moment * rows, rows)
        combined = strengths[moment, 0:1, 0:1] * below[place].astype(jnp.float32) + strengths[
            moment, 1:2, 0:1
        ] * above[place].astype(jnp.float32)
        energy_in[place] = jnp.where(live_rows, combined, jnp.zeros((), jnp.float32)).astype(
            jnp.bfloat16
        )

    def out_copy(moment, place):
        return pltpu.make_async_remote_copy(
            src_ref=fresh.at[moment],
            dst_ref=out_ref.at[0, 0, row_block(place)],
            send_sem=out_send.at[moment],
            recv_sem=out_recv.at[place],
            device_id={"tm": moment},
            device_id_type=MESH,
        )

    running = jnp.zeros((rows, states), jnp.float32)
    for moment in range(times):
        depth = (times - moment) * rows
        product = jnp.dot(
            energy_in[0:depth], history[moment], preferred_element_type=jnp.float32
        )
        if moment == 0:
            sums[...] = product
        else:
            sums[moment * rows : states] += product
        running = decay * running + step_size * sums[moment * rows : (moment + 1) * rows]
        free_part = jnp.where(
            shown, jnp.exp(-rates * (moment * step_size)), jnp.zeros((), jnp.float32)
        )
        fresh[moment] = (free_part - step_size * running).astype(jnp.bfloat16)

        @pl.when(me != moment)
        def _():
            out_copy(moment, me).start()

        @pl.when(me == moment)
        def _():
            out_ref[0, 0, row_block(me)] = fresh[moment]

    for mask in range(1, times):
        pltpu.make_async_remote_copy(
            src_ref=fresh.at[0],
            dst_ref=out_ref.at[0, 0, row_block(flipped(me, mask))],
            send_sem=out_send.at[0],
            recv_sem=out_recv.at[flipped(me, mask)],
            device_id={"tm": flipped(me, mask)},
            device_id_type=MESH,
        ).wait_recv()
    for moment in range(times):

        @pl.when(me != moment)
        def _():
            out_copy(moment, me).wait_send()

    for mask in range(1, times):
        strength_copy(mask, me).wait_send()
        for part in range(PARTS):
            gather_copy(mask, part, flipped(me, mask)).wait_send()

    @pl.when(has_below)
    def _():
        share_copy(my_half).wait_send()
        for mask in range(times):
            down_copy(mask).wait_send()

    @pl.when(has_above)
    def _():
        operator_copy().wait_send()
        for mask in range(times):
            up_copy(mask).wait_send()


def fused_device(propagator, rising_op, energies, hyb_particle, hyb_hole, sector_sizes):
    times = lax.axis_size("tm")
    states = propagator.shape[-1]
    square = (states, states)
    narrow, wide = jnp.bfloat16, jnp.float32
    vmem = pl.BlockSpec(memory_space=pltpu.VMEM)
    smem = pl.BlockSpec(memory_space=pltpu.SMEM)
    dma = pltpu.SemaphoreType.DMA
    return pl.pallas_call(
        functools.partial(fused_kernel, times, lax.axis_size("sector")),
        out_shape=jax.ShapeDtypeStruct(propagator.shape, narrow),
        in_specs=[smem, smem, smem, vmem, vmem, vmem],
        out_specs=vmem,
        scratch_shapes=[
            pltpu.VMEM((times,) + square, narrow),
            pltpu.VMEM(square, narrow),
            pltpu.VMEM(square, narrow),
            pltpu.VMEM((2 * (states // times), states), narrow),
            pltpu.VMEM(square, narrow),
            pltpu.VMEM(square, narrow),
            pltpu.VMEM(square, narrow),
            pltpu.VMEM(square, narrow),
            pltpu.VMEM(square, narrow),
            pltpu.VMEM(square, wide),
            pltpu.VMEM((times, states // times, states), narrow),
            pltpu.VMEM((times, SUBLANES, LANES), wide),
            dma((2,)),
            dma((2,)),
            dma((times,)),
            dma((times,)),
            dma((times,)),
            dma((times,)),
            dma((times, PARTS)),
            dma((times, PARTS)),
            dma((times,)),
            dma((times,)),
            dma((times,)),
            dma((times,)),
        ],
        compiler_params=pltpu.CompilerParams(
            collective_id=0, has_side_effects=True, vmem_limit_bytes=28 * 2**20
        ),
    )(sector_sizes, hyb_particle, hyb_hole, propagator, rising_op, energies)


def per_device(propagator, rising_op, energies, hyb_particle, hyb_hole, sector_sizes):
    times = lax.axis_size("tm")
    states = propagator.shape[-1]
    fits = (
        propagator.shape[1] == 1
        and times > 2
        and times & (times - 1) == 0
        and states % (times * ROW_TILE) == 0
        and states % (PARTS * ROW_TILE) == 0
        and states % LANES == 0
    )
    chosen = fused_device if fits else general_device
    return chosen(propagator, rising_op, energies, hyb_particle, hyb_hole, sector_sizes)


def solution(mesh):
    placed = (
        P("sector", "tm", None, None),
        P("sector", None, None),
        P("sector", None),
        P("tm"),
        P("tm"),
        P("sector"),
    )
    return jax.shard_map(
        per_device,
        mesh=mesh,
        in_specs=placed,
        out_specs=P("sector", "tm", None, None),
        check_vma=False,
    )
```
